256 devices in a mesh: grp: 2 (over core), tx: 8 (over y, x_lo), ty: 16 (over z, x_hi).
Axes of the slice: x: 4 (x_hi: 2, x_lo: 2; x = x_hi * 2 + x_lo), y: 4, z: 8, core: 2. Of those that a mesh axis runs over, the one named last changes fastest.
Arguments:
- endpoints: float32 [2, 5, 16, 64, 2048], P('grp', None, None, 'tx', 'ty'), may hold values from -4 to 5, as said below
Outputs:
- adjoints: float32 [2, 5, 16, 64, 2048], P('grp', None, None, 'tx', 'ty')
- forward_states: float32 [2, 5, 16, 64, 2048], P('grp', None, None, 'tx', 'ty')
The draws below stay inside these ranges and needn't reach their ends.
Inputs may be any that keep to these rules, and one draw needn't show every extreme that they name: `endpoints`: in entry 0 the density lies in 1 to 2, each velocity component (momentum over density) in -0.5 to 0.5 and the pressure 0.4 (E - |m|^2 / (2 density)) in 0.5 to 1.5; entry 1 is a cotangent within -4 to 4.
All inputs are finite; a program needn't handle non-finite values.
Results may differ from the reference program's by a relative error of at most 0.00002.
Values sent between devices are 32-bit elements; how exact they have to be, the bound alone decides.
A program may use at most 64 MiB of HBM per device.

```python
import jax
import jax.numpy as jnp

NZ = 16
NX = 64
NY = 2048


gas_gamma = 1.4


def draw_endpoints(key, part):
    keys = jax.random.split(jax.random.fold_in(key, 17), 5)
    grid_shape = (NZ, NX, NY)
    density = jax.random.uniform(keys[0], grid_shape, jnp.float32, 1.0, 2.0)
    cotangent = jnp.clip(jax.random.normal(keys[3], (5,) + grid_shape, jnp.float32), -4.0, 4.0)
    velocity = jax.random.uniform(keys[1], (3,) + grid_shape, jnp.float32, -0.5, 0.5)
    pressure = jax.random.uniform(keys[2], grid_shape, jnp.float32, 0.5, 1.5)
    momentum = density[None] * velocity
    energy = pressure / (gas_gamma - 1.0) + 0.5 * density * jnp.sum(velocity * velocity, axis=0)
    fields = jnp.concatenate([density[None], momentum, energy[None]], axis=0)
    return jnp.stack([fields, cotangent])


def setup_inputs(seed: int = 0) -> dict:
    arg_keys = jax.random.split(jax.random.key(seed), 2)
    return {
        "endpoints": draw_endpoints(jax.random.fold_in(arg_keys[1], 71), 0),
    }


gas_gamma = 1.4
time_step = 0.05
viscosity = 0.1
directions = ((1, 2), (2, 3), (3, 1))

def euler_flux(fields, component):
    density = fields[0]
    inverse = 1.0 / density
    kinetic = 0.5 * inverse * (fields[1] * fields[1] + fields[2] * fields[2] + fields[3] * fields[3])
    pressure = (gas_gamma - 1.0) * (fields[4] - kinetic)
    velocity = fields[component] * inverse
    components = [fields[component], fields[1] * velocity, fields[2] * velocity, fields[3] * velocity, (fields[4] + pressure) * velocity]
    components[component] = components[component] + pressure
    return jnp.stack(components)

def rate_field(fields):
    tendency = jnp.zeros_like(fields)
    for component, spatial in directions:
        fluxes = euler_flux(fields, component)
        tendency = tendency - 0.5 * (jnp.roll(fluxes, -1, spatial) - jnp.roll(fluxes, 1, spatial))
        tendency = tendency + viscosity * (jnp.roll(fields, -1, spatial) + jnp.roll(fields, 1, spatial) - 2.0 * fields)
    return tendency

def heun_step(fields):
    first_rate = rate_field(fields)
    section_state = fields + time_step * first_rate
    return fields + 0.5 * time_step * (first_rate + rate_field(section_state))

def reference(endpoints):
    initial = endpoints[0]
    final_cot = endpoints[1]
    midway = heun_step(initial)
    ending = heun_step(midway)
    outputs, pullback = jax.vjp(heun_step, midway)
    middle_cot, = pullback(final_cot)
    outputs, pullback = jax.vjp(heun_step, initial)
    start_cot, = pullback(middle_cot)
    return (jnp.stack([start_cot, middle_cot]), jnp.stack([midway, ending]))
```

```python
import jax
import jax.numpy as jnp
from jax import lax
from jax.experimental import pallas as pl
from jax.experimental.pallas import tpu as pltpu
from jax.sharding import PartitionSpec as P

time_step = 0.05
viscosity = 0.1
ROWS, PLANES, LANES = 8, 16, 128
MESH = pl.DeviceIdType.MESH
LEFT, RIGHT, UP_LEFT, UP_RIGHT, DOWN_LEFT, DOWN_RIGHT, OWN = range(7)
FROM_UP, FROM_DOWN, CENTRE = 7, 8, 9


def half_fluxes(v):
    density, m1, m2, m3, energy = v
    half = 0.5 / density
    h1, h2, h3 = (m1 * half, m2 * half, m3 * half)
    a11, a22, a33 = (m1 * h1, m2 * h2, m3 * h3)
    a12, a13, a23 = (m1 * h2, m1 * h3, m2 * h3)
    pressure = 0.4 * (energy - (a11 + a22 + a33))
    hp = 0.5 * pressure
    enthalpy = energy + pressure
    return (
        (0.5 * m1, a11 + hp, a12, a13, enthalpy * h1),
        (0.5 * m2, a12, a22 + hp, a23, enthalpy * h2),
        (0.5 * m3, a13, a23, a33 + hp, enthalpy * h3),
    )


def pulled_back(v, w, diffusion):
    density, m1, m2, m3, energy = v
    inverse = 1.0 / density
    u = (m1 * inverse, m2 * inverse, m3 * inverse)
    square = u[0] * u[0] + u[1] * u[1] + u[2] * u[2]
    pressure = 0.4 * (energy - 0.5 * density * square)
    enthalpy = (energy + pressure) * inverse
    q = w[0][4] * u[0] + w[1][4] * u[1] + w[2][4] * u[2]
    cp = w[0][1] + w[1][2] + w[2][3] + q
    s01 = w[0][2] + w[1][1]
    s02 = w[0][3] + w[2][1]
    s12 = w[1][3] + w[2][2]
    t = (
        2.0 * w[0][1] * u[0] + s01 * u[1] + s02 * u[2],
        s01 * u[0] + 2.0 * w[1][2] * u[1] + s12 * u[2],
        s02 * u[0] + s12 * u[1] + 2.0 * w[2][3] * u[2],
    )
    c4 = 0.4 * cp
    out = [
        0.5 * c4 * square - 0.5 * (t[0] * u[0] + t[1] * u[1] + t[2] * u[2]) - q * enthalpy
    ]
    for k in range(3):
        out.append(w[k][0] + t[k] + w[k][4] * enthalpy - c4 * u[k])
    out.append(q + c4)
    return [0.5 * out[f] + viscosity * diffusion[f] for f in range(5)]


def kernel(
    x_ref, adj_ref, st_ref,
    ea, eb, ec, outb, pk, pr, sbuf, wbuf, rsu, rsl, sst, wst,
    gxp, gxm, tbuf, gyp, gym, send_sem, recv_sem,
):
    grp = lax.axis_index("grp")
    tx = lax.axis_index("tx")
    ty = lax.axis_index("ty")
    ntx = lax.axis_size("tx")
    nty = lax.axis_size("ty")
    txs = {-1: lax.rem(tx + ntx - 1, ntx), 0: tx, 1: lax.rem(tx + 1, ntx)}
    tys = {-1: lax.rem(ty + nty - 1, nty), 0: ty, 1: lax.rem(ty + 1, nty)}

    lane = lax.broadcasted_iota(jnp.int32, (PLANES, LANES), 1)

    barrier = pltpu.get_barrier_semaphore()
    for g in (grp, 1 - grp):
        for dx in (-1, 0, 1):
            for dy in (-1, 0, 1):
                if dx == 0 and dy == 0:
                    continue
                pl.semaphore_signal(
                    barrier, inc=1, device_id=(g, txs[dx], tys[dy]), device_id_type=MESH
                )
    pl.semaphore_signal(barrier, inc=1, device_id=(1 - grp, tx, ty), device_id_type=MESH)

    ext = (ea, eb, ec)

    def copies(phase):
        target = grp if phase == 0 else 1 - grp
        if phase == 0:
            rows_low, rows_high = (ea.at[:, 2:4], ea.at[:, 8:10])
        else:
            rows_low, rows_high = (outb.at[:, 0:2], outb.at[:, 6:8])

        def make(k, src, dst, dx, dy):
            return pltpu.make_async_remote_copy(
                src_ref=src,
                dst_ref=dst,
                send_sem=send_sem.at[phase, k],
                recv_sem=recv_sem.at[phase, k],
                device_id=(target, txs[dx], tys[dy]),
                device_id_type=MESH,
            )

        result = []
        for k, dx, dy in (
            (UP_LEFT, 1, 1), (UP_RIGHT, 1, -1), (DOWN_LEFT, -1, 1), (DOWN_RIGHT, -1, -1),
            (LEFT, 0, 1), (RIGHT, 0, -1),
        ):
            result.append(make(k, pk.at[phase], pr.at[phase, k], dx, dy))
        result.append(make(FROM_UP, rows_high, ext[phase].at[:, 0:2], 1, 0))
        result.append(make(FROM_DOWN, rows_low, ext[phase].at[:, 10:12], -1, 0))
        if phase:
            result.append(make(OWN, pk.at[phase], pr.at[phase, OWN], 0, 0))
            result.append(make(CENTRE, outb, ext[phase].at[:, 2:10], 0, 0))
        return result

    def pack(phase, row):
        packed = None
        for f in range(5):
            q = None
            for r in range(ROWS):
                moved = pltpu.roll(row(f, r), (16 * r + 2 + 4 * (f % 4)) % LANES, 1)
                q = moved if q is None else jnp.where(lane >= 16 * r, moved, q)
            if f < 4:
                packed = q if f == 0 else jnp.where(lane % 16 >= 4 * f, q, packed)
            else:
                pk[phase, 1] = q
        pk[phase, 0] = packed

    def unpack(phase, rs):
        low = lane % 4 < 2
        for a in range(2):
            own = pk[phase, a] if phase == 0 else pr[phase, OWN, a]
            first = jnp.where(low, pr[phase, LEFT, a], own)
            second = jnp.where(low, own, pr[phase, RIGHT, a])
            before = lane >= 112
            after = lane < 16
            parts = (
                (jnp.where(before, pr[phase, UP_LEFT, a], first),
                 jnp.where(before, pr[phase, UP_RIGHT, a], second), 16),
                (first, second, 0),
                (jnp.where(after, pr[phase, DOWN_LEFT, a], first),
                 jnp.where(after, pr[phase, DOWN_RIGHT, a], second), LANES - 16),
            )
            for b, (one, two, shift) in enumerate(parts):
                for f in range(4) if a == 0 else (4,):
                    base = shift - 4 * (f % 4)
                    rs[f, b] = jnp.where(
                        lane % 16 < 8,
                        pltpu.roll(one, (base + 2 * LANES) % LANES, 1),
                        pltpu.roll(two, (base + 8 + 2 * LANES) % LANES, 1),
                    )

    def y_minus(value, edge, r):
        return jnp.where(lane == 0, pltpu.roll(edge, 127 - 16 * r, 1), pltpu.roll(value, 1, 1))

    def y_plus(value, edge, r):
        return jnp.where(
            lane == LANES - 1, pltpu.roll(edge, 117 - 16 * r, 1), pltpu.roll(value, LANES - 1, 1)
        )

    def z_minus(value):
        return pltpu.roll(value, 1, 0)

    def z_plus(value):
        return pltpu.roll(value, PLANES - 1, 0)

    def which(row):
        block = (row >= 0).astype(jnp.int32) + (row >= ROWS).astype(jnp.int32)
        return block, jnp.clip(row, 0, ROWS - 1)

    def rate_rows(src, count, finish):
        for i, out in ((0, gxm), (count - 1, gxp)):
            v = [src[f, i] for f in range(5)]
            flux = half_fluxes(v)[0]
            for f in range(5):
                out[f, i] = viscosity * v[f] + (flux[f] if i == 0 else -flux[f])

        def local(i, carry):
            if count == ROWS + 4:
                block, place = which(i - 2)
            else:
                block, place = (1, i - 1)
            v = [src[f, i] for f in range(5)]
            fx, fy, fz = half_fluxes(v)
            for f in range(5):
                damped = viscosity * v[f]
                gxp[f, i] = damped - fx[f]
                gxm[f, i] = damped + fx[f]
                tbuf[f, i] = (
                    y_minus(damped + fy[f], gym[f, block], place)
                    + y_plus(damped - fy[f], gyp[f, block], place)
                    + (z_minus(damped + fz[f]) + z_plus(damped - fz[f]) - 6.0 * damped)
                )
            return carry

        lax.fori_loop(1, count - 1, local, 0)

        def gather(i, carry):
            finish(i, [tbuf[f, i] + gxp[f, i + 1] + gxm[f, i - 1] for f in range(5)])
            return carry

        lax.fori_loop(1, count - 1, gather, 0)

    def section(e, rs):
        tend = None
        for b in range(3):
            v = [rs[f, b] for f in range(5)]
            fx, fy, fz = half_fluxes(v)
            terms = []
            for f in range(5):
                damped = viscosity * v[f]
                minus, plus = (damped + fy[f], damped - fy[f])
                gym[f, b] = minus
                gyp[f, b] = plus
                if b == 1:
                    terms.append(
                        pltpu.roll(minus, 1, 1) + pltpu.roll(plus, LANES - 1, 1)
                        + z_minus(damped + fz[f]) + z_plus(damped - fz[f]) - 6.0 * damped
                    )
                else:
                    terms.append(damped + fx[f] if b == 0 else damped - fx[f])
            tend = terms if tend is None else [x + y for x, y in zip(tend, terms)]
        for f in range(5):
            sst[f] = rs[f, 1] + time_step * tend[f]

        def finish(i, rate):
            for f in range(5):
                sbuf[f, i - 1] = e[f, i] + time_step * rate[f]

        rate_rows(e, ROWS + 4, finish)

    def advance(e, store):
        v = [sst[f] for f in range(5)]
        fy = half_fluxes(v)[1]
        for f in range(5):
            gym[f, 1] = viscosity * v[f] + fy[f]
            gyp[f, 1] = viscosity * v[f] - fy[f]

        def finish(i, rate):
            store(i - 1, [
                0.5 * (e[f, i + 1] + sbuf[f, i]) + (0.5 * time_step) * rate[f] for f in range(5)
            ])

        rate_rows(sbuf, ROWS + 2, finish)

    def adjoint_at(v, centre, pairs):
        w = [[plus - minus for minus, plus in pairs[d]] for d in range(3)]
        diffusion = [
            sum(pairs[d][f][0] + pairs[d][f][1] for d in range(3)) - 6.0 * centre[f]
            for f in range(5)
        ]
        return pulled_back(v, w, diffusion)

    def weigh(centre, pulled):
        return (0.5 * time_step) * centre + (0.5 * time_step * time_step) * pulled

    def section_adjoint(e, rs):
        centre = [rs[f, 1] for f in range(5)]
        pulled = adjoint_at(
            [sst[f] for f in range(5)],
            centre,
            (
                [(rs[f, 0], rs[f, 2]) for f in range(5)],
                [(pltpu.roll(c, 1, 1), pltpu.roll(c, LANES - 1, 1)) for c in centre],
                [(z_minus(c), z_plus(c)) for c in centre],
            ),
        )
        for f in range(5):
            wst[f] = weigh(centre[f], pulled[f])

        def body(i, carry):
            block, place = which(i - 1)
            centre = [e[f, i + 1] for f in range(5)]
            pulled = adjoint_at(
                [sbuf[f, i] for f in range(5)],
                centre,
                (
                    [(e[f, i], e[f, i + 2]) for f in range(5)],
                    [
                        (y_minus(centre[f], rs[f, block], place), y_plus(centre[f], rs[f, block], place))
                        for f in range(5)
                    ],
                    [(z_minus(c), z_plus(c)) for c in centre],
                ),
            )
            for f in range(5):
                wbuf[f, i] = weigh(centre[f], pulled[f])
            return carry

        lax.fori_loop(0, ROWS + 2, body, 0)

    def state_adjoint(eu, el, store):
        def body(r, carry):
            centre = [wbuf[f, r + 1] for f in range(5)]
            pulled = adjoint_at(
                [eu[f, r + 2] for f in range(5)],
                centre,
                (
                    [(wbuf[f, r], wbuf[f, r + 2]) for f in range(5)],
                    [(y_minus(centre[f], wst[f], r), y_plus(centre[f], wst[f], r)) for f in range(5)],
                    [(z_minus(c), z_plus(c)) for c in centre],
                ),
            )
            store(r, [
                0.5 * el[f, r + 2] + (1.0 / time_step) * centre[f] + pulled[f] for f in range(5)
            ])
            return carry

        lax.fori_loop(0, ROWS, body, 0)

    def tile_row(f, r):
        return pl.ds(f * ROWS * PLANES + r, PLANES, stride=ROWS)

    def into(ref, send):
        def store(r, values):
            for f in range(5):
                ref[tile_row(f, r), :] = values[f]
                if send:
                    outb[f, r] = values[f]
        return store

    for f in range(5):
        for r in range(ROWS):
            ea[f, 2 + r] = x_ref[tile_row(f, r), :]
    pack(0, lambda f, r: ea[f, 2 + r])

    pl.semaphore_wait(barrier, 17)
    first = copies(0)
    for copy in first:
        copy.start()
    for copy in first:
        copy.wait_recv()

    @pl.when(grp == 0)
    def _():
        unpack(0, rsu)
        section(ea, rsu)
        advance(ea, into(st_ref, True))
        pack(1, lambda f, r: outb[f, r])
        second = copies(1)
        for copy in second:
            copy.start()
        third = copies(2)
        for copy in third:
            copy.wait_recv()
        unpack(2, rsl)
        section_adjoint(ec, rsl)
        state_adjoint(ea, ec, into(adj_ref, False))
        for copy in second:
            copy.wait_send()

    @pl.when(grp == 1)
    def _():
        unpack(0, rsl)
        for copy in copies(1):
            copy.wait_recv()
        unpack(1, rsu)
        section(eb, rsu)
        section_adjoint(ea, rsl)
        state_adjoint(eb, ea, into(adj_ref, True))
        pack(2, lambda f, r: outb[f, r])
        third = copies(2)
        for copy in third:
            copy.start()
        advance(eb, into(st_ref, False))
        for copy in third:
            copy.wait_send()

    for copy in first:
        copy.wait_send()


def shards(endpoints):
    flat = endpoints.reshape(5 * PLANES * ROWS, LANES)
    vmem = pl.BlockSpec(memory_space=pltpu.VMEM)
    plane = (PLANES, LANES)

    def buf(*lead):
        return pltpu.VMEM((*lead, *plane), jnp.float32)

    adjoints, states = pl.pallas_call(
        kernel,
        out_shape=(jax.ShapeDtypeStruct(flat.shape, jnp.float32),) * 2,
        in_specs=[vmem],
        out_specs=(vmem, vmem),
        scratch_shapes=[
            buf(5, 12), buf(5, 12), buf(5, 12),
            buf(5, 8),
            buf(3, 2), buf(3, 7, 2),
            buf(5, 10), buf(5, 10),
            buf(5, 3), buf(5, 3),
            buf(5), buf(5),
            buf(5, 12), buf(5, 12), buf(5, 12),
            buf(5, 3), buf(5, 3),
            pltpu.SemaphoreType.DMA((3, 10)),
            pltpu.SemaphoreType.DMA((3, 10)),
        ],
        compiler_params=pltpu.CompilerParams(collective_id=0, has_side_effects=True),
    )(flat)
    return (adjoints.reshape(endpoints.shape), states.reshape(endpoints.shape))


def solution(mesh):
    spec = P("grp", None, None, "tx", "ty")
    return jax.shard_map(
        shards, mesh=mesh, in_specs=(spec,), out_specs=(spec, spec), check_vma=False
    )
```

```python
import jax
import jax.numpy as jnp
from jax import lax
from jax.experimental import pallas as pl
from jax.experimental.pallas import tpu as pltpu
from jax.sharding import PartitionSpec as P

time_step = 0.05
viscosity = 0.1
ROWS, PLANES, LANES = 8, 16, 128
MESH = pl.DeviceIdType.MESH
LEFT, RIGHT, UP_LEFT, UP_RIGHT, DOWN_LEFT, DOWN_RIGHT, OWN = range(7)
FROM_UP, FROM_DOWN, CENTRE = 7, 8, 9


def half_fluxes(v):
    density, m1, m2, m3, energy = v
    half = 0.5 / density
    h1, h2, h3 = (m1 * half, m2 * half, m3 * half)
    a11, a22, a33 = (m1 * h1, m2 * h2, m3 * h3)
    a12, a13, a23 = (m1 * h2, m1 * h3, m2 * h3)
    pressure = 0.4 * (energy - (a11 + a22 + a33))
    hp = 0.5 * pressure
    enthalpy = energy + pressure
    return (
        (0.5 * m1, a11 + hp, a12, a13, enthalpy * h1),
        (0.5 * m2, a12, a22 + hp, a23, enthalpy * h2),
        (0.5 * m3, a13, a23, a33 + hp, enthalpy * h3),
    )


def pulled_back(v, w, diffusion):
    density, m1, m2, m3, energy = v
    inverse = 1.0 / density
    u = (m1 * inverse, m2 * inverse, m3 * inverse)
    square = u[0] * u[0] + u[1] * u[1] + u[2] * u[2]
    pressure = 0.4 * (energy - 0.5 * density * square)
    enthalpy = (energy + pressure) * inverse
    q = w[0][4] * u[0] + w[1][4] * u[1] + w[2][4] * u[2]
    cp = w[0][1] + w[1][2] + w[2][3] + q
    s01 = w[0][2] + w[1][1]
    s02 = w[0][3] + w[2][1]
    s12 = w[1][3] + w[2][2]
    t = (
        2.0 * w[0][1] * u[0] + s01 * u[1] + s02 * u[2],
        s01 * u[0] + 2.0 * w[1][2] * u[1] + s12 * u[2],
        s02 * u[0] + s12 * u[1] + 2.0 * w[2][3] * u[2],
    )
    c4 = 0.4 * cp
    out = [
        0.5 * c4 * square - 0.5 * (t[0] * u[0] + t[1] * u[1] + t[2] * u[2]) - q * enthalpy
    ]
    for k in range(3):
        out.append(w[k][0] + t[k] + w[k][4] * enthalpy - c4 * u[k])
    out.append(q + c4)
    return [0.5 * out[f] + viscosity * diffusion[f] for f in range(5)]


def kernel(
    x_hbm, adj_ref, st_ref,
    x_ref,
    ea, eb, ec, outb, pk, pr, sbuf, wbuf, rsu, rsl, sst, wst,
    gxp, gxm, tbuf, gyp, gym, send_sem, recv_sem, load_sem, ready,
):
    grp = lax.axis_index("grp")
    tx = lax.axis_index("tx")
    ty = lax.axis_index("ty")
    ntx = lax.axis_size("tx")
    nty = lax.axis_size("ty")
    txs = {-1: lax.rem(tx + ntx - 1, ntx), 0: tx, 1: lax.rem(tx + 1, ntx)}
    tys = {-1: lax.rem(ty + nty - 1, nty), 0: ty, 1: lax.rem(ty + 1, nty)}

    lane = lax.broadcasted_iota(jnp.int32, (PLANES, LANES), 1)

    barrier = pltpu.get_barrier_semaphore()
    for dy in (-1, 1, 0):
        for dx in (-1, 1, 0):
            g = 1 - grp if dx == 0 and dy == 0 else grp
            pl.semaphore_signal(
                barrier, inc=1, device_id=(g, txs[dx], tys[dy]), device_id_type=MESH
            )
    load = pltpu.make_async_copy(x_hbm, x_ref, load_sem)
    load.start()
    load.wait()

    ext = (ea, eb, ec)

    def copies(phase):
        target = grp if phase == 0 else 1 - grp
        if phase == 0:
            rows_low, rows_high = (ea.at[:, 2:4], ea.at[:, 8:10])
        else:
            rows_low, rows_high = (outb.at[:, 0:2], outb.at[:, 6:8])

        def make(k, src, dst, dx, dy):
            return pltpu.make_async_remote_copy(
                src_ref=src,
                dst_ref=dst,
                send_sem=send_sem.at[phase, k],
                recv_sem=recv_sem.at[phase, k],
                device_id=(target, txs[dx], tys[dy]),
                device_id_type=MESH,
            )

        result = []
        for k, dx, dy in (
            (UP_LEFT, 1, 1), (UP_RIGHT, 1, -1), (DOWN_LEFT, -1, 1), (DOWN_RIGHT, -1, -1),
            (LEFT, 0, 1), (RIGHT, 0, -1),
        ):
            result.append(make(k, pk.at[phase], pr.at[phase, k], dx, dy))
        result.append(make(FROM_UP, rows_high, ext[phase].at[:, 0:2], 1, 0))
        result.append(make(FROM_DOWN, rows_low, ext[phase].at[:, 10:12], -1, 0))
        if phase:
            result.append(make(OWN, pk.at[phase], pr.at[phase, OWN], 0, 0))
            result.append(make(CENTRE, outb, ext[phase].at[:, 2:10], 0, 0))
        return result

    def pack(phase, row):
        packed = None
        for f in range(5):
            q = None
            for r in range(ROWS):
                moved = pltpu.roll(row(f, r), (16 * r + 2 + 4 * (f % 4)) % LANES, 1)
                q = moved if q is None else jnp.where(lane >= 16 * r, moved, q)
            if f < 4:
                packed = q if f == 0 else jnp.where(lane % 16 >= 4 * f, q, packed)
            else:
                pk[phase, 1] = q
        pk[phase, 0] = packed

    def unpack(phase, rs):
        low = lane % 4 < 2
        for a in range(2):
            own = pk[phase, a] if phase == 0 else pr[phase, OWN, a]
            first = jnp.where(low, pr[phase, LEFT, a], own)
            second = jnp.where(low, own, pr[phase, RIGHT, a])
            before = lane >= 112
            after = lane < 16
            parts = (
                (jnp.where(before, pr[phase, UP_LEFT, a], first),
                 jnp.where(before, pr[phase, UP_RIGHT, a], second), 16),
                (first, second, 0),
                (jnp.where(after, pr[phase, DOWN_LEFT, a], first),
                 jnp.where(after, pr[phase, DOWN_RIGHT, a], second), LANES - 16),
            )
            for b, (one, two, shift) in enumerate(parts):
                for f in range(4) if a == 0 else (4,):
                    base = shift - 4 * (f % 4)
                    rs[f, b] = jnp.where(
                        lane % 16 < 8,
                        pltpu.roll(one, (base + 2 * LANES) % LANES, 1),
                        pltpu.roll(two, (base + 8 + 2 * LANES) % LANES, 1),
                    )

    def y_minus(value, edge, r):
        return jnp.where(lane == 0, pltpu.roll(edge, 127 - 16 * r, 1), pltpu.roll(value, 1, 1))

    def y_plus(value, edge, r):
        return jnp.where(
            lane == LANES - 1, pltpu.roll(edge, 117 - 16 * r, 1), pltpu.roll(value, LANES - 1, 1)
        )

    def z_minus(value):
        return pltpu.roll(value, 1, 0)

    def z_plus(value):
        return pltpu.roll(value, PLANES - 1, 0)

    def which(row):
        block = (row >= 0).astype(jnp.int32) + (row >= ROWS).astype(jnp.int32)
        return block, jnp.clip(row, 0, ROWS - 1)

    def rate_rows(src, count, finish):
        for i, out in ((0, gxm), (count - 1, gxp)):
            v = [src[f, i] for f in range(5)]
            flux = half_fluxes(v)[0]
            for f in range(5):
                out[f, i] = viscosity * v[f] + (flux[f] if i == 0 else -flux[f])

        def local(i, carry):
            if count == ROWS + 4:
                block, place = which(i - 2)
            else:
                block, place = (1, i - 1)
            v = [src[f, i] for f in range(5)]
            fx, fy, fz = half_fluxes(v)
            for f in range(5):
                damped = viscosity * v[f]
                gxp[f, i] = damped - fx[f]
                gxm[f, i] = damped + fx[f]
                tbuf[f, i] = (
                    y_minus(damped + fy[f], gym[f, block], place)
                    + y_plus(damped - fy[f], gyp[f, block], place)
                    + (z_minus(damped + fz[f]) + z_plus(damped - fz[f]) - 6.0 * damped)
                )
            return carry

        lax.fori_loop(1, count - 1, local, 0, unroll=True)

        def gather(i, carry):
            finish(i, [tbuf[f, i] + gxp[f, i + 1] + gxm[f, i - 1] for f in range(5)])
            return carry

        lax.fori_loop(1, count - 1, gather, 0, unroll=True)

    def section(e, rs):
        tend = None
        for b in range(3):
            v = [rs[f, b] for f in range(5)]
            fx, fy, fz = half_fluxes(v)
            terms = []
            for f in range(5):
                damped = viscosity * v[f]
                minus, plus = (damped + fy[f], damped - fy[f])
                gym[f, b] = minus
                gyp[f, b] = plus
                if b == 1:
                    terms.append(
                        pltpu.roll(minus, 1, 1) + pltpu.roll(plus, LANES - 1, 1)
                        + z_minus(damped + fz[f]) + z_plus(damped - fz[f]) - 6.0 * damped
                    )
                else:
                    terms.append(damped + fx[f] if b == 0 else damped - fx[f])
            tend = terms if tend is None else [x + y for x, y in zip(tend, terms)]
        for f in range(5):
            sst[f] = rs[f, 1] + time_step * tend[f]

        def finish(i, rate):
            for f in range(5):
                sbuf[f, i - 1] = e[f, i] + time_step * rate[f]

        rate_rows(e, ROWS + 4, finish)

    def advance(e, store):
        v = [sst[f] for f in range(5)]
        fy = half_fluxes(v)[1]
        for f in range(5):
            gym[f, 1] = viscosity * v[f] + fy[f]
            gyp[f, 1] = viscosity * v[f] - fy[f]

        def finish(i, rate):
            store(i - 1, [
                0.5 * (e[f, i + 1] + sbuf[f, i]) + (0.5 * time_step) * rate[f] for f in range(5)
            ])

        rate_rows(sbuf, ROWS + 2, finish)

    def adjoint_at(v, centre, pairs):
        w = [[plus - minus for minus, plus in pairs[d]] for d in range(3)]
        diffusion = [
            sum(pairs[d][f][0] + pairs[d][f][1] for d in range(3)) - 6.0 * centre[f]
            for f in range(5)
        ]
        return pulled_back(v, w, diffusion)

    def weigh(centre, pulled):
        return (0.5 * time_step) * centre + (0.5 * time_step * time_step) * pulled

    def section_adjoint(e, rs):
        centre = [rs[f, 1] for f in range(5)]
        pulled = adjoint_at(
            [sst[f] for f in range(5)],
            centre,
            (
                [(rs[f, 0], rs[f, 2]) for f in range(5)],
                [(pltpu.roll(c, 1, 1), pltpu.roll(c, LANES - 1, 1)) for c in centre],
                [(z_minus(c), z_plus(c)) for c in centre],
            ),
        )
        for f in range(5):
            wst[f] = weigh(centre[f], pulled[f])

        def body(i, carry):
            block, place = which(i - 1)
            centre = [e[f, i + 1] for f in range(5)]
            pulled = adjoint_at(
                [sbuf[f, i] for f in range(5)],
                centre,
                (
                    [(e[f, i], e[f, i + 2]) for f in range(5)],
                    [
                        (y_minus(centre[f], rs[f, block], place), y_plus(centre[f], rs[f, block], place))
                        for f in range(5)
                    ],
                    [(z_minus(c), z_plus(c)) for c in centre],
                ),
            )
            for f in range(5):
                wbuf[f, i] = weigh(centre[f], pulled[f])
            return carry

        lax.fori_loop(0, ROWS + 2, body, 0, unroll=True)

    def state_adjoint(eu, el, store):
        def body(r, carry):
            centre = [wbuf[f, r + 1] for f in range(5)]
            pulled = adjoint_at(
                [eu[f, r + 2] for f in range(5)],
                centre,
                (
                    [(wbuf[f, r], wbuf[f, r + 2]) for f in range(5)],
                    [(y_minus(centre[f], wst[f], r), y_plus(centre[f], wst[f], r)) for f in range(5)],
                    [(z_minus(c), z_plus(c)) for c in centre],
                ),
            )
            store(r, [
                0.5 * el[f, r + 2] + (1.0 / time_step) * centre[f] + pulled[f] for f in range(5)
            ])
            return carry

        lax.fori_loop(0, ROWS, body, 0, unroll=True)

    def tile_row(f, r):
        return pl.ds(f * ROWS * PLANES + r, PLANES, stride=ROWS)

    def into(ref, send):
        def store(r, values):
            for f in range(5):
                ref[tile_row(f, r), :] = values[f]
                if send:
                    outb[f, r] = values[f]
        return store

    for f in range(5):
        for r in range(ROWS):
            ea[f, 2 + r] = x_ref[tile_row(f, r), :]
    pack(0, lambda f, r: ea[f, 2 + r])

    pl.semaphore_wait(barrier, 9)
    first = copies(0)
    for copy in first:
        copy.start()
    pl.semaphore_signal(ready, inc=1, device_id=(1 - grp, tx, ty), device_id_type=MESH)
    pl.semaphore_wait(ready, 1)
    for copy in first:
        copy.wait_recv()

    @pl.when(grp == 0)
    def _():
        unpack(0, rsu)
        section(ea, rsu)
        advance(ea, into(st_ref, True))
        pack(1, lambda f, r: outb[f, r])
        second = copies(1)
        for copy in second:
            copy.start()
        third = copies(2)
        for copy in third:
            copy.wait_recv()
        unpack(2, rsl)
        section_adjoint(ec, rsl)
        state_adjoint(ea, ec, into(adj_ref, False))
        for copy in second:
            copy.wait_send()

    @pl.when(grp == 1)
    def _():
        unpack(0, rsl)
        for copy in copies(1):
            copy.wait_recv()
        unpack(1, rsu)
        section(eb, rsu)
        section_adjoint(ea, rsl)
        state_adjoint(eb, ea, into(adj_ref, True))
        pack(2, lambda f, r: outb[f, r])
        third = copies(2)
        for copy in third:
            copy.start()
        advance(eb, into(st_ref, False))
        for copy in third:
            copy.wait_send()

    for copy in first:
        copy.wait_send()


def put_out(adj_ref, st_ref, adj_out, st_out, sems):
    moves = (
        pltpu.make_async_copy(adj_ref, adj_out, sems.at[0]),
        pltpu.make_async_copy(st_ref, st_out, sems.at[1]),
    )
    for move in moves:
        move.start()
    for move in moves:
        move.wait()


def shards(endpoints):
    flat = endpoints.reshape(5 * PLANES * ROWS, LANES)
    vmem = pl.BlockSpec(memory_space=pltpu.VMEM)
    plane = (PLANES, LANES)

    def buf(*lead):
        return pltpu.VMEM((*lead, *plane), jnp.float32)

    adjoints, states = pl.pallas_call(
        kernel,
        out_shape=(pltpu.VMEM(flat.shape, jnp.float32),) * 2,
        in_specs=[pl.BlockSpec(memory_space=pl.ANY)],
        out_specs=(vmem, vmem),
        scratch_shapes=[
            pltpu.VMEM(flat.shape, jnp.float32),
            buf(5, 12), buf(5, 12), buf(5, 12),
            buf(5, 8),
            buf(3, 2), buf(3, 7, 2),
            buf(5, 10), buf(5, 10),
            buf(5, 3), buf(5, 3),
            buf(5), buf(5),
            buf(5, 12), buf(5, 12), buf(5, 12),
            buf(5, 3), buf(5, 3),
            pltpu.SemaphoreType.DMA((3, 10)),
            pltpu.SemaphoreType.DMA((3, 10)),
            pltpu.SemaphoreType.DMA,
            pltpu.SemaphoreType.REGULAR,
        ],
        compiler_params=pltpu.CompilerParams(collective_id=0, has_side_effects=True),
    )(flat)
    anywhere = pl.BlockSpec(memory_space=pl.ANY)
    adjoints, states = pl.pallas_call(
        put_out,
        out_shape=(jax.ShapeDtypeStruct(flat.shape, jnp.float32),) * 2,
        in_specs=[vmem, vmem],
        out_specs=(anywhere, anywhere),
        scratch_shapes=[pltpu.SemaphoreType.DMA((2,))],
    )(*(pltpu.with_memory_space_constraint(a, pltpu.VMEM) for a in (adjoints, states)))
    return (adjoints.reshape(endpoints.shape), states.reshape(endpoints.shape))


def solution(mesh):
    spec = P("grp", None, None, "tx", "ty")
    return jax.shard_map(
        shards, mesh=mesh, in_specs=(spec,), out_specs=(spec, spec), check_vma=False
    )
```

```python
import jax
import jax.numpy as jnp
from jax import lax
from jax.experimental import pallas as pl
from jax.experimental.pallas import tpu as pltpu
from jax.sharding import PartitionSpec as P

time_step = 0.05
viscosity = 0.1
ROWS, PLANES, LANES = 8, 16, 128
MESH = pl.DeviceIdType.MESH
LEFT, RIGHT, UP_LEFT, UP_RIGHT, DOWN_LEFT, DOWN_RIGHT, OWN = range(7)
FROM_UP, FROM_DOWN, CENTRE = 7, 8, 9


def half_fluxes(v):
    density, m1, m2, m3, energy = v
    half = 0.5 / density
    h1, h2, h3 = (m1 * half, m2 * half, m3 * half)
    a11, a22, a33 = (m1 * h1, m2 * h2, m3 * h3)
    a12, a13, a23 = (m1 * h2, m1 * h3, m2 * h3)
    pressure = 0.4 * (energy - (a11 + a22 + a33))
    hp = 0.5 * pressure
    enthalpy = energy + pressure
    return (
        (0.5 * m1, a11 + hp, a12, a13, enthalpy * h1),
        (0.5 * m2, a12, a22 + hp, a23, enthalpy * h2),
        (0.5 * m3, a13, a23, a33 + hp, enthalpy * h3),
    )


def pulled_back(v, w, diffusion):
    density, m1, m2, m3, energy = v
    inverse = 1.0 / density
    u = (m1 * inverse, m2 * inverse, m3 * inverse)
    square = u[0] * u[0] + u[1] * u[1] + u[2] * u[2]
    pressure = 0.4 * (energy - 0.5 * density * square)
    enthalpy = (energy + pressure) * inverse
    q = w[0][4] * u[0] + w[1][4] * u[1] + w[2][4] * u[2]
    cp = w[0][1] + w[1][2] + w[2][3] + q
    s01 = w[0][2] + w[1][1]
    s02 = w[0][3] + w[2][1]
    s12 = w[1][3] + w[2][2]
    t = (
        2.0 * w[0][1] * u[0] + s01 * u[1] + s02 * u[2],
        s01 * u[0] + 2.0 * w[1][2] * u[1] + s12 * u[2],
        s02 * u[0] + s12 * u[1] + 2.0 * w[2][3] * u[2],
    )
    c4 = 0.4 * cp
    out = [
        0.5 * c4 * square - 0.5 * (t[0] * u[0] + t[1] * u[1] + t[2] * u[2]) - q * enthalpy
    ]
    for k in range(3):
        out.append(w[k][0] + t[k] + w[k][4] * enthalpy - c4 * u[k])
    out.append(q + c4)
    return [0.5 * out[f] + viscosity * diffusion[f] for f in range(5)]


def kernel(
    x_hbm, adj_ref, st_ref,
    x_ref,
    ea, eb, ec, outb, pk, pr, sbuf, wbuf, rsu, rsl, sst, wst,
    gxp, gxm, tbuf, gedge, wys, wzs, seconds, send_sem, recv_sem, load_sem, ready,
):
    grp = lax.axis_index("grp")
    tx = lax.axis_index("tx")
    ty = lax.axis_index("ty")
    ntx = lax.axis_size("tx")
    nty = lax.axis_size("ty")
    txs = {-1: lax.rem(tx + ntx - 1, ntx), 0: tx, 1: lax.rem(tx + 1, ntx)}
    tys = {-1: lax.rem(ty + nty - 1, nty), 0: ty, 1: lax.rem(ty + 1, nty)}

    lane = lax.broadcasted_iota(jnp.int32, (PLANES, LANES), 1)

    barrier = pltpu.get_barrier_semaphore()
    for dy in (-1, 1, 0):
        for dx in (-1, 1, 0):
            g = 1 - grp if dx == 0 and dy == 0 else grp
            pl.semaphore_signal(
                barrier, inc=1, device_id=(g, txs[dx], tys[dy]), device_id_type=MESH
            )
    load = pltpu.make_async_copy(x_hbm, x_ref, load_sem)
    load.start()
    load.wait()

    ext = (ea, eb, ec)

    def copies(phase):
        target = grp if phase == 0 else 1 - grp
        if phase == 0:
            rows_low, rows_high = (ea.at[:, 2:4], ea.at[:, 8:10])
        else:
            rows_low, rows_high = (outb.at[:, 0:2], outb.at[:, 6:8])

        def make(k, src, dst, dx, dy):
            return pltpu.make_async_remote_copy(
                src_ref=src,
                dst_ref=dst,
                send_sem=send_sem.at[phase, k],
                recv_sem=recv_sem.at[phase, k],
                device_id=(target, txs[dx], tys[dy]),
                device_id_type=MESH,
            )

        result = []
        for k, dx, dy in (
            (UP_LEFT, 1, 1), (UP_RIGHT, 1, -1), (DOWN_LEFT, -1, 1), (DOWN_RIGHT, -1, -1),
            (LEFT, 0, 1), (RIGHT, 0, -1),
        ):
            result.append(make(k, pk.at[phase], pr.at[phase, k], dx, dy))
        result.append(make(FROM_UP, rows_high, ext[phase].at[:, 0:2], 1, 0))
        result.append(make(FROM_DOWN, rows_low, ext[phase].at[:, 10:12], -1, 0))
        if phase:
            result.append(make(OWN, pk.at[phase], pr.at[phase, OWN], 0, 0))
            result.append(make(CENTRE, outb, ext[phase].at[:, 2:10], 0, 0))
        return result

    def pack(phase, row):
        packed = None
        for f in range(5):
            q = None
            for r in range(ROWS):
                moved = pltpu.roll(row(f, r), (16 * r + 2 + 4 * (f % 4)) % LANES, 1)
                q = moved if q is None else jnp.where(lane >= 16 * r, moved, q)
            if f < 4:
                packed = q if f == 0 else jnp.where(lane % 16 >= 4 * f, q, packed)
            else:
                pk[phase, 1] = q
        pk[phase, 0] = packed

    def unpack(phase, rs):
        low = lane % 4 < 2
        for a in range(2):
            own = pk[phase, a] if phase == 0 else pr[phase, OWN, a]
            first = jnp.where(low, pr[phase, LEFT, a], own)
            second = jnp.where(low, own, pr[phase, RIGHT, a])
            before = lane >= 112
            after = lane < 16
            parts = (
                (jnp.where(before, pr[phase, UP_LEFT, a], first),
                 jnp.where(before, pr[phase, UP_RIGHT, a], second), 16),
                (first, second, 0),
                (jnp.where(after, pr[phase, DOWN_LEFT, a], first),
                 jnp.where(after, pr[phase, DOWN_RIGHT, a], second), LANES - 16),
            )
            for b, (one, two, shift) in enumerate(parts):
                for f in range(4) if a == 0 else (4,):
                    base = shift - 4 * (f % 4)
                    rs[f, b] = jnp.where(
                        lane % 16 < 8,
                        pltpu.roll(one, (base + 2 * LANES) % LANES, 1),
                        pltpu.roll(two, (base + 8 + 2 * LANES) % LANES, 1),
                    )

    both_ends = (lane == 0) | (lane == LANES - 1)

    def joined(before, after):
        return jnp.where(lane % 16 == 0, pltpu.roll(after, LANES - 10, 1), before)

    def edge_row(pairs, r):
        return pltpu.roll(pairs, 127 - 16 * r, 1)

    def y_minus(value, edge):
        return jnp.where(lane == 0, edge, pltpu.roll(value, 1, 1))

    def y_plus(value, edge):
        return jnp.where(lane == LANES - 1, edge, pltpu.roll(value, LANES - 1, 1))

    def z_minus(value):
        return pltpu.roll(value, 1, 0)

    def z_plus(value):
        return pltpu.roll(value, PLANES - 1, 0)

    def x_terms(src, count):
        for i, out in ((0, gxm), (count - 1, gxp)):
            v = [src[f, i] for f in range(5)]
            flux = half_fluxes(v)[0]
            for f in range(5):
                out[f, i] = viscosity * v[f] + (flux[f] if i == 0 else -flux[f])

    def local(src, i, edge):
        v = [src[f, i] for f in range(5)]
        fx, fy, fz = half_fluxes(v)
        for f in range(5):
            damped = viscosity * v[f]
            gxp[f, i] = damped - fx[f]
            gxm[f, i] = damped + fx[f]
            ends = edge(f)
            tbuf[f, i] = (
                y_minus(damped + fy[f], ends)
                + y_plus(damped - fy[f], ends)
                + (z_minus(damped + fz[f]) + z_plus(damped - fz[f]) - 6.0 * damped)
            )

    def section_inside(e):
        for i in range(2, ROWS + 2):
            local(e, i, lambda f: 0.0)

    def section(e, rs):
        tend = None
        for b in range(3):
            v = [rs[f, b] for f in range(5)]
            fx, fy, fz = half_fluxes(v)
            terms = []
            for f in range(5):
                damped = viscosity * v[f]
                minus, plus = (damped + fy[f], damped - fy[f])
                gedge[f, b] = joined(minus, plus)
                if b == 1:
                    terms.append(
                        pltpu.roll(minus, 1, 1) + pltpu.roll(plus, LANES - 1, 1)
                        + z_minus(damped + fz[f]) + z_plus(damped - fz[f]) - 6.0 * damped
                    )
                else:
                    terms.append(damped + fx[f] if b == 0 else damped - fx[f])
            tend = terms if tend is None else [x + y for x, y in zip(tend, terms)]
        for f in range(5):
            sst[f] = rs[f, 1] + time_step * tend[f]
        x_terms(e, ROWS + 4)
        local(e, 1, lambda f: edge_row(gedge[f, 0], 0))
        local(e, ROWS + 2, lambda f: edge_row(gedge[f, 2], ROWS - 1))
        for i in range(1, ROWS + 3):
            for f in range(5):
                rate = tbuf[f, i] + gxp[f, i + 1] + gxm[f, i - 1]
                if 2 <= i < ROWS + 2:
                    rate = rate + jnp.where(both_ends, edge_row(gedge[f, 1], i - 2), 0.0)
                sbuf[f, i - 1] = e[f, i] + time_step * rate

    def advance(e, store):
        v = [sst[f] for f in range(5)]
        fy = half_fluxes(v)[1]
        for f in range(5):
            gedge[f, 1] = joined(viscosity * v[f] + fy[f], viscosity * v[f] - fy[f])
        x_terms(sbuf, ROWS + 2)
        for i in range(1, ROWS + 1):
            local(sbuf, i, lambda f: edge_row(gedge[f, 1], i - 1))
        for i in range(1, ROWS + 1):
            store(i - 1, [
                0.5 * (e[f, i + 1] + sbuf[f, i])
                + (0.5 * time_step) * (tbuf[f, i] + gxp[f, i + 1] + gxm[f, i - 1])
                for f in range(5)
            ])

    def yz_terms(centre, edge):
        ends = [edge(f) for f in range(5)]
        y = [(y_minus(c, end), y_plus(c, end)) for c, end in zip(centre, ends)]
        z = [(z_minus(c), z_plus(c)) for c in centre]
        return (
            [plus - minus for minus, plus in y],
            [plus - minus for minus, plus in z],
            [y[f][0] + y[f][1] + z[f][0] + z[f][1] - 6.0 * centre[f] for f in range(5)],
        )

    def apply(v, x_pairs, yz):
        wy, wz, second = yz
        return pulled_back(
            v,
            [[plus - minus for minus, plus in x_pairs], wy, wz],
            [second[f] + x_pairs[f][0] + x_pairs[f][1] for f in range(5)],
        )

    def weigh(centre, pulled):
        return (0.5 * time_step) * centre + (0.5 * time_step * time_step) * pulled

    def save_yz(e, i, edge):
        parts = yz_terms([e[f, i + 1] for f in range(5)], edge)
        for f in range(5):
            wys[f, i] = parts[0][f]
            wzs[f, i] = parts[1][f]
            seconds[f, i] = parts[2][f]

    def differences_inside(e):
        for i in range(1, ROWS + 1):
            save_yz(e, i, lambda f: 0.0)

    def differences(e, rs):
        pairs = [[joined(rs[f, b], rs[f, b]) for f in range(5)] for b in (0, 2)]
        save_yz(e, 0, lambda f: edge_row(pairs[0][f], 0))
        save_yz(e, ROWS + 1, lambda f: edge_row(pairs[1][f], ROWS - 1))
        for f in range(5):
            middle = joined(rs[f, 1], rs[f, 1])
            for i in range(1, ROWS + 1):
                ends = jnp.where(both_ends, edge_row(middle, i - 1), 0.0)
                wys[f, i] = wys[f, i] + jnp.where(lane == 0, -ends, ends)
                seconds[f, i] = seconds[f, i] + ends

    def section_adjoint(e, rs):
        centre = [rs[f, 1] for f in range(5)]
        z = [(z_minus(c), z_plus(c)) for c in centre]
        y = [(pltpu.roll(c, 1, 1), pltpu.roll(c, LANES - 1, 1)) for c in centre]
        pulled = apply(
            [sst[f] for f in range(5)],
            [(rs[f, 0], rs[f, 2]) for f in range(5)],
            (
                [plus - minus for minus, plus in y],
                [plus - minus for minus, plus in z],
                [y[f][0] + y[f][1] + z[f][0] + z[f][1] - 6.0 * centre[f] for f in range(5)],
            ),
        )
        for f in range(5):
            wst[f] = weigh(centre[f], pulled[f])
        for i in range(ROWS + 2):
            pulled = apply(
                [sbuf[f, i] for f in range(5)],
                [(e[f, i], e[f, i + 2]) for f in range(5)],
                tuple([ref[f, i] for f in range(5)] for ref in (wys, wzs, seconds)),
            )
            for f in range(5):
                wbuf[f, i] = weigh(e[f, i + 1], pulled[f])

    def state_adjoint(eu, el, store):
        pairs = [joined(wst[f], wst[f]) for f in range(5)]
        for r in range(ROWS):
            centre = [wbuf[f, r + 1] for f in range(5)]
            pulled = apply(
                [eu[f, r + 2] for f in range(5)],
                [(wbuf[f, r], wbuf[f, r + 2]) for f in range(5)],
                yz_terms(centre, lambda f: edge_row(pairs[f], r)),
            )
            store(r, [
                0.5 * el[f, r + 2] + (1.0 / time_step) * centre[f] + pulled[f] for f in range(5)
            ])

    def tile_row(f, r):
        return pl.ds(f * ROWS * PLANES + r, PLANES, stride=ROWS)

    def into(ref, send):
        def store(r, values):
            for f in range(5):
                ref[tile_row(f, r), :] = values[f]
                if send:
                    outb[f, r] = values[f]
        return store

    for f in range(5):
        for r in range(ROWS):
            ea[f, 2 + r] = x_ref[tile_row(f, r), :]
    pack(0, lambda f, r: ea[f, 2 + r])

    pl.semaphore_wait(barrier, 9)
    first = copies(0)
    for copy in first:
        copy.start()
    pl.semaphore_signal(ready, inc=1, device_id=(1 - grp, tx, ty), device_id_type=MESH)

    @pl.when(grp == 0)
    def _():
        section_inside(ea)
        for copy in first:
            copy.wait_recv()
        unpack(0, rsu)
        section(ea, rsu)
        advance(ea, into(st_ref, True))
        pack(1, lambda f, r: outb[f, r])
        pl.semaphore_wait(ready, 1)
        second = copies(1)
        for copy in second:
            copy.start()
        third = copies(2)
        third[-1].wait_recv()
        differences_inside(ec)
        for copy in third[:-1]:
            copy.wait_recv()
        unpack(2, rsl)
        differences(ec, rsl)
        section_adjoint(ec, rsl)
        state_adjoint(ea, ec, into(adj_ref, False))
        for copy in second:
            copy.wait_send()

    @pl.when(grp == 1)
    def _():
        differences_inside(ea)
        for copy in first:
            copy.wait_recv()
        unpack(0, rsl)
        differences(ea, rsl)
        second = copies(1)
        second[-1].wait_recv()
        section_inside(eb)
        for copy in second[:-1]:
            copy.wait_recv()
        unpack(1, rsu)
        section(eb, rsu)
        section_adjoint(ea, rsl)
        state_adjoint(eb, ea, into(adj_ref, True))
        pack(2, lambda f, r: outb[f, r])
        pl.semaphore_wait(ready, 1)
        third = copies(2)
        for copy in third:
            copy.start()
        advance(eb, into(st_ref, False))
        for copy in third:
            copy.wait_send()

    for copy in first:
        copy.wait_send()


def put_out(adj_ref, st_ref, adj_out, st_out, sems):
    moves = (
        pltpu.make_async_copy(adj_ref, adj_out, sems.at[0]),
        pltpu.make_async_copy(st_ref, st_out, sems.at[1]),
    )
    for move in moves:
        move.start()
    for move in moves:
        move.wait()


def shards(endpoints):
    flat = endpoints.reshape(5 * PLANES * ROWS, LANES)
    vmem = pl.BlockSpec(memory_space=pltpu.VMEM)
    plane = (PLANES, LANES)

    def buf(*lead):
        return pltpu.VMEM((*lead, *plane), jnp.float32)

    adjoints, states = pl.pallas_call(
        kernel,
        out_shape=(pltpu.VMEM(flat.shape, jnp.float32),) * 2,
        in_specs=[pl.BlockSpec(memory_space=pl.ANY)],
        out_specs=(vmem, vmem),
        scratch_shapes=[
            pltpu.VMEM(flat.shape, jnp.float32),
            buf(5, 12), buf(5, 12), buf(5, 12),
            buf(5, 8),
            buf(3, 2), buf(3, 7, 2),
            buf(5, 10), buf(5, 10),
            buf(5, 3), buf(5, 3),
            buf(5), buf(5),
            buf(5, 12), buf(5, 12), buf(5, 12),
            buf(5, 3),
            buf(5, 10), buf(5, 10), buf(5, 10),
            pltpu.SemaphoreType.DMA((3, 10)),
            pltpu.SemaphoreType.DMA((3, 10)),
            pltpu.SemaphoreType.DMA,
            pltpu.SemaphoreType.REGULAR,
        ],
        compiler_params=pltpu.CompilerParams(collective_id=0, has_side_effects=True),
    )(flat)
    anywhere = pl.BlockSpec(memory_space=pl.ANY)
    adjoints, states = pl.pallas_call(
        put_out,
        out_shape=(jax.ShapeDtypeStruct(flat.shape, jnp.float32),) * 2,
        in_specs=[vmem, vmem],
        out_specs=(anywhere, anywhere),
        scratch_shapes=[pltpu.SemaphoreType.DMA((2,))],
    )(*(pltpu.with_memory_space_constraint(a, pltpu.VMEM) for a in (adjoints, states)))
    return (adjoints.reshape(endpoints.shape), states.reshape(endpoints.shape))


def solution(mesh):
    spec = P("grp", None, None, "tx", "ty")
    return jax.shard_map(
        shards, mesh=mesh, in_specs=(spec,), out_specs=(spec, spec), check_vma=False
    )
```
